256 devices in a mesh: row: 8 (over z), col: 16 (over x_hi, y, core), rep: 2 (over x_lo).
Axes of the slice: x: 4 (x_hi: 2, x_lo: 2; x = x_hi * 2 + x_lo), y: 4, z: 8, core: 2. Of those that a mesh axis runs over, the one named last changes fastest.
Arguments:
- descriptors: float32 [2048, 256], P('rep', 'col'), may hold values from -6 to 6
- landmarks: float32 [12288, 256], P('row', 'col'), may hold values from -6 to 6
- whitening: float32 [12288, 12288], P('row', 'col'), may hold values from -1 to 1
- assign: int32 [2048], replicated, may hold values from 0 to 4095
Outputs:
- cluster_sums: float32 [4096, 12288], P(('row', 'rep'), 'col')
The draws below stay inside these ranges and needn't reach their ends.
All inputs are finite; a program needn't handle non-finite values.
Results may differ from the reference program's by a relative error of at most 0.00016.
Values sent between devices are 32-bit elements; how exact they have to be, the bound alone decides.
A program may use at most 64 MiB of HBM per device.

```python
import jax
import jax.numpy as jnp
from jax import lax

FEATURES = 256
SPREAD = 51
LANDMARKS = 12288
CLUSTERS = 4096
ROWS = 2048


latent_dims = 16


def feature_points(key, salt, row_count):
    salted = jax.random.fold_in(key, salt)
    latent_key = jax.random.fold_in(salted, 101)
    jitter_key = jax.random.fold_in(salted, 202)
    latent = jax.random.truncated_normal(latent_key, -4.0, 4.0, (row_count, latent_dims), jnp.float32)
    jitter = jax.random.truncated_normal(jitter_key, -4.0, 4.0, (row_count, FEATURES), jnp.float32)
    latent_index = jnp.arange(FEATURES, dtype=jnp.int32) % latent_dims
    return jnp.take(latent, latent_index, axis=1) + 0.5 * jitter


def draw_descriptors(key, part):
    return feature_points(key, 1, ROWS)


def draw_landmarks(key, part):
    return feature_points(key, 2, LANDMARKS)


def set_ends(result, rng, low, high):
    index_at = [jax.random.randint(jax.random.fold_in(rng, axis), (), 0, length) for axis, length in enumerate(result.shape)]
    longest = result.shape.index(max(result.shape))
    neighbour = index_at[:longest] + [(index_at[longest] + 1) % result.shape[longest]] + index_at[longest + 1:]
    return result.at[tuple(index_at)].set(low).at[tuple(neighbour)].set(high)


def shard_levels(key, extent, cuts, least, high):
    def one(axis_at, shards_of):
        steps = jax.random.uniform(jax.random.fold_in(jax.random.fold_in(key, 6), axis_at), (shards_of,), jnp.float32, least / len(cuts), high / len(cuts))
        return jnp.repeat(jnp.exp(steps), extent[axis_at] // shards_of).reshape((-1,) + (1,) * (len(extent) - axis_at - 1))

    level = one(*cuts[0])
    for cut in cuts[1:]:
        level = level * one(*cut)
    return level


def gaussian(rng, extent, deviation, limit, shards=(), held_as=jnp.bfloat16):
    drawn = jax.random.normal(rng, extent, jnp.float32) * deviation
    if len(shards) > 0:
        drawn = shard_levels(rng, extent, shards, -0.22, 0.18) * drawn
    return jnp.clip(drawn, min=-limit, max=limit).astype(held_as)


def setup_inputs(seed: int = 0) -> dict:
    seeds = jax.random.split(jax.random.key(seed), 5)
    return {
        "descriptors": draw_descriptors(jax.random.fold_in(seeds[4], 71), 0),
        "landmarks": draw_landmarks(jax.random.fold_in(seeds[4], 71), 0),
        "whitening": gaussian(seeds[2], (LANDMARKS, LANDMARKS), (max(1, LANDMARKS // 400)) ** -0.5, 1.0, ((0, 8), (1, 16)), jnp.float32),
        "assign": set_ends(jax.random.randint(seeds[3], (ROWS,), 0, CLUSTERS), jax.random.fold_in(seeds[3], 1), 0, CLUSTERS - 1).astype(jnp.int32),
    }


def reference(descriptors, landmarks, whitening, assign):
    highest = lax.Precision.HIGHEST
    row_square = jnp.sum(descriptors * descriptors, axis=1)
    centre_square = jnp.sum(landmarks * landmarks, axis=1)
    inner = jnp.dot(descriptors, landmarks.T, precision=highest, preferred_element_type=jnp.float32)
    distance = row_square[:, None] + centre_square[None, :] - 2.0 * inner
    kernel = jnp.exp(-distance / (2.0 * SPREAD))
    whitened = jnp.dot(kernel, whitening, precision=highest, preferred_element_type=jnp.float32)
    return jax.ops.segment_sum(whitened, assign, num_segments=CLUSTERS)
```

```python
import functools

import jax
import jax.numpy as jnp
from jax import lax
from jax.experimental import pallas as pl
from jax.experimental.pallas import tpu as pltpu
from jax.sharding import PartitionSpec as P

SPREAD = 51
CLUSTERS = 4096

f32, bf16 = jnp.float32, jnp.bfloat16
MESH = pl.DeviceIdType.MESH


def nn(a, b):
    return lax.dot_general(a, b, (((1,), (0,)), ((), ())), preferred_element_type=f32)


def nt(a, b):
    return lax.dot_general(a, b, (((1,), (1,)), ((), ())), preferred_element_type=f32)


def split(x):
    high = x.astype(bf16)
    return high, (x - high.astype(f32)).astype(bf16)


def ones_where(mask):
    return jnp.where(mask, 1.0, 0.0).astype(bf16)


def iota(shape, axis):
    return lax.broadcasted_iota(jnp.int32, shape, axis)


def kernel(slots, dense, points_ref, centres_ref, white_ref, assign_ref, out_ref,
           feats, wfull, wh, wl, dh, dl, lh, ll, pick, fold, pos, kh, kl, ah, al,
           sbuf, rbuf, local_sem, gs, gr, fs, fr, zs, zr):
    rows = assign_ref.shape[1]
    part = points_ref.shape[1]
    centres = centres_ref.shape[1]
    cols = white_ref.shape[1]
    owned = out_ref.shape[0]
    half = slots // 2
    z, c, p = lax.axis_index("row"), lax.axis_index("col"), lax.axis_index("rep")
    nz = lax.axis_size("row")
    xh, y, core = c // 8, lax.rem(c // 2, 4), lax.rem(c, 2)
    sibling = {"row": z, "col": c + 1 - 2 * core, "rep": p}
    ahead = {"row": lax.rem(z + 1, nz), "col": c, "rep": p}
    behind = {"row": lax.rem(z + nz - 1, nz), "col": c, "rep": p}

    def slot(col, rep, both):
        start = rep * part if both else rep * (part + centres)
        return feats.at[pl.ds(pl.multiple_of(col * 16, 16), 16),
                        pl.ds(pl.multiple_of(start, 128), part + centres if both else part)]

    def peer(a, b, dy):
        px = a + xh - 2 * a * xh
        return px * 8 + lax.rem(y + dy, 4) * 2 + core, b + p - 2 * b * p

    own_points = pltpu.make_async_copy(points_ref, slot(c, p, False), local_sem.at[0])
    own_centres = pltpu.make_async_copy(
        centres_ref, feats.at[pl.ds(pl.multiple_of(c * 16, 16), 16), pl.ds(part, centres)], local_sem.at[1])
    own_white = pltpu.make_async_copy(white_ref, wfull, local_sem.at[2])
    own_points.start()
    own_centres.start()
    own_white.start()

    barrier = pltpu.get_barrier_semaphore()
    others = [(a, b, dy) for dy in range(4) for a in range(2) for b in range(2) if (a, b, dy) != (0, 0, 0)]
    for a, b, dy in others:
        col, rep = peer(a, b, dy)
        pl.semaphore_signal(barrier, inc=1, device_id={"row": z, "col": col, "rep": rep}, device_id_type=MESH)
    for target in (sibling, ahead, behind):
        pl.semaphore_signal(barrier, inc=1, device_id=target, device_id_type=MESH)
    pl.semaphore_wait(barrier, len(others) + 3)

    own_points.wait()
    own_centres.wait()

    def gather(a, b, dy):
        index = (a * 2 + b) * 4 + dy
        col, rep = peer(a, b, dy)
        mine = slot(c, p, a == b)
        return pltpu.make_async_remote_copy(mine, mine, gs.at[index], gr.at[index],
                                            device_id={"row": z, "col": col, "rep": rep}, device_id_type=MESH)

    def arrival(a, b, dy, both):
        index = (a * 2 + b) * 4 + dy
        col, rep = peer(a, b, 4 - dy)
        theirs = slot(col, rep, both)
        return (pltpu.make_async_remote_copy(theirs, theirs, gs.at[index], gr.at[index],
                                             device_id=sibling, device_id_type=MESH),
                pltpu.make_async_remote_copy(theirs, theirs, fs.at[index], fr.at[index],
                                             device_id=sibling, device_id_type=MESH))

    def handed(a, b, dy, both):
        index = (a * 2 + b) * 4 + dy
        col, rep = peer(a, b, 4 - dy)
        theirs = slot(col + 1 - 2 * core, rep, both)
        return pltpu.make_async_remote_copy(theirs, theirs, fs.at[index], fr.at[index],
                                            device_id=sibling, device_id_type=MESH)

    for a, b, dy in others:
        gather(a, b, dy).start()
    arrival(0, 0, 0, True)[1].start()

    own_white.wait()

    @pl.loop(0, centres // 128)
    def _(i):
        at = pl.ds(pl.multiple_of(i * 128, 128), 128)
        high, low = split(wfull[at, :])
        wh[at, :] = high
        wl[at, :] = low

    assign = assign_ref[...]
    owner_of = assign // owned

    def owner_at(j):
        far = nz // 2 - (j + 1) // 2
        step = jnp.where(lax.rem(j, 2) == 1, far, nz - far) if not isinstance(j, int) else (far if j % 2 else nz - far)
        return lax.rem(z + step, nz) * 2 + p

    def members(owner):
        return ones_where(iota((owned, rows), 0) == assign - owner * owned)

    if not dense:
        before = ones_where(iota((128, 128), 0) < iota((128, 128), 1))
        base = jnp.zeros((16, 1), f32)
        for block in range(rows // 128):
            at = pl.ds(block * 128, 128)
            mine = ones_where(iota((16, 128), 0) == owner_of[:, block * 128:(block + 1) * 128])
            mine32 = mine.astype(f32)
            pos[:, at] = jnp.sum(mine32 * (nn(mine, before) + base), axis=0, keepdims=True)
            base = base + jnp.sum(mine32, axis=1, keepdims=True)
        below = ones_where(iota((owned, owned), 0) < iota((owned, owned), 1))

    def prepare(j):
        owner = owner_at(j)
        take = fold.shape[2]
        rank = jnp.where(owner_of == owner, pos[...], -1.0).astype(jnp.int32)
        chosen = ones_where(iota((take, rows), 0) == rank)
        pick[j] = chosen
        belongs = members(owner)
        counts = nt(jnp.ones((8, rows), bf16), belongs)
        active = counts > 0.5
        order = nn(ones_where(active), below).astype(jnp.int32)
        squeeze = ones_where((iota((slots, owned), 0) == order[0:1]) & active[0:1])
        fold[j] = nn(squeeze, nt(belongs, chosen).astype(bf16)).astype(bf16)

    def pass_on(j):
        dy = lax.rem(j, 4)
        a = j // 4

        @pl.when(j > 0)
        def _():
            got, on = arrival(a, a, dy, True)
            got.wait_recv()
            on.start()

        got, on = arrival(a, 1 - a, dy, False)
        got.wait_recv()
        on.start()

    @pl.loop(0, 8)
    def _(j):
        if not dense:
            prepare(j)
        pass_on(j)

    @pl.loop(0, 8)
    def _(j):
        dy = lax.rem(j, 4)
        a = j // 4
        handed(a, a, dy, True).wait_recv()
        handed(a, 1 - a, dy, False).wait_recv()

    squares = jnp.zeros((1, centres), f32)
    for i in range(8):
        at = pl.ds(i * 32, 32)
        centre = feats[at, part:part + centres]
        squares = squares + jnp.sum(centre * centre, axis=0, keepdims=True)
        lh[at, :], ll[at, :] = split(centre)
        dh[at, :part], dl[at, :part] = split(feats[at, :part])
        dh[at, part:], dl[at, part:] = split(feats[at, part + centres:])

    def kernel_rows(xhi, xlo, at):
        x = xhi + xlo
        norm = jnp.sum(x * x, axis=1, keepdims=True)
        xhi, xlo = xhi.astype(bf16), xlo.astype(bf16)
        for i in range(centres // 512):
            on = slice(i * 512, (i + 1) * 512)
            inner = nn(xhi, lh[:, on]) + nn(xhi, ll[:, on]) + nn(xlo, lh[:, on])
            value = jnp.exp((norm + squares[:, on] - 2.0 * inner) * (-1.0 / (2.0 * SPREAD)))
            kh[at, on], kl[at, on] = split(value)

    if dense:
        eye = ones_where(iota((256, 256), 0) == iota((256, 256), 1))

        @pl.loop(0, rows // 256)
        def _(i):
            at = pl.ds(pl.multiple_of(i * 256, 256), 256)
            kernel_rows(nt(eye, dh[:, at]), nt(eye, dl[:, at]), at)

    def blocks(first, count):
        if not dense:
            take = fold.shape[2]
            for i in range(count):
                chosen = pick[first + i]
                kernel_rows(nt(chosen, dh[...]), nt(chosen, dl[...]), slice(i * take, (i + 1) * take))
        for i in range(count):
            at = slice(i * slots, (i + 1) * slots)
            if dense:
                chosen, on = members(owner_at(first + i)), slice(0, rows)
            else:
                chosen, on = fold[first + i], slice(i * take, (i + 1) * take)
            for k in range(centres // 512):
                lanes = slice(k * 512, (k + 1) * 512)
                ah[at, lanes], al[at, lanes] = split(nn(chosen, kh[on, lanes]) + nn(chosen, kl[on, lanes]))
        every = slice(0, count * slots)
        return nn(ah[every, :], wh[...]) + nn(ah[every, :], wl[...]) + nn(al[every, :], wh[...])

    def hop(way, step, part_of):
        at = pl.ds(part_of * half, half)
        return pltpu.make_async_remote_copy(sbuf.at[way, step, at], rbuf.at[way, step, at],
                                            zs.at[way, step, part_of], zr.at[way, step, part_of],
                                            device_id=(ahead, behind)[way], device_id_type=MESH)

    made = blocks(0, 1)
    sbuf[0, 0, :half] = made[:half]
    sbuf[1, 0, half:] = made[half:]
    hop(0, 0, 0).start()
    hop(1, 0, 1).start()
    for step in range(1, 4):
        made = blocks(2 * step - 1, 2)
        sbuf[0, step] = made[:slots]
        sbuf[1, step] = made[slots:]
        for turn in range(2):
            for way in range(2):
                part_of = (1 - way if turn == 0 else way) if step == 1 else turn
                at = pl.ds(part_of * half, half)
                if step > 1 or turn == 1:
                    hop(way, step - 1, part_of).wait_recv()
                    sbuf[way, step, at] += rbuf[way, step - 1, at]
                hop(way, step, part_of).start()
    made = blocks(7, 1)
    if not dense:
        belongs = members(lax.rem(z, nz) * 2 + p)
        counts = nn(belongs, jnp.ones((rows, slots), bf16))
        order = nn(ones_where(iota((owned, owned), 0) > iota((owned, owned), 1)), ones_where(counts > 0.5))
        spread = ones_where((order.astype(jnp.int32) == iota((owned, slots), 1)) & (counts > 0.5))
    for way in range(2):
        for part_of in range(2):
            hop(way, 3, part_of).wait_recv()
    total = made + rbuf[0, 3] + rbuf[1, 3]
    if dense:
        out_ref[...] = total
    else:
        high, low = split(total)
        rest = (total - high.astype(f32) - low.astype(f32)).astype(bf16)
        out_ref[...] = nn(spread, high) + nn(spread, low) + nn(spread, rest)

    for a, b, dy in others:
        gather(a, b, dy).wait_send()
    for j in range(8):
        a, dy = j // 4, j % 4
        arrival(a, a, dy, True)[1].wait_send()
        arrival(a, 1 - a, dy, False)[1].wait_send()
    for way in range(2):
        for step in range(4):
            for part_of in range(2):
                if step > 0 or part_of == way:
                    hop(way, step, part_of).wait_send()


def call(slots, take, dense, points, centres, white, assign):
    features, part = points.shape[0] * lax.axis_size("col"), points.shape[1]
    count, cols = white.shape
    rows = assign.shape[1]
    owned = CLUSTERS // (lax.axis_size("row") * lax.axis_size("rep"))
    held = rows if dense else 2 * take
    dma = pltpu.SemaphoreType.DMA
    small = dense
    return pl.pallas_call(
        functools.partial(kernel, slots, dense),
        out_shape=jax.ShapeDtypeStruct((owned, cols), f32),
        in_specs=[pl.BlockSpec(memory_space=pl.ANY)] * 3 + [pl.BlockSpec(memory_space=pltpu.VMEM)],
        out_specs=pl.BlockSpec(memory_space=pltpu.VMEM),
        scratch_shapes=[
            pltpu.VMEM((features, 2 * part + count), f32),
            pltpu.VMEM((count, cols), f32),
            pltpu.VMEM((count, cols), bf16),
            pltpu.VMEM((count, cols), bf16),
            pltpu.VMEM((features, rows), bf16),
            pltpu.VMEM((features, rows), bf16),
            pltpu.VMEM((features, count), bf16),
            pltpu.VMEM((features, count), bf16),
            pltpu.VMEM((8, 16, 128) if small else (8, take, rows), bf16),
            pltpu.VMEM((8, 16, 128) if small else (8, slots, take), bf16),
            pltpu.VMEM((1, rows), f32),
            pltpu.VMEM((held, count), bf16),
            pltpu.VMEM((held, count), bf16),
            pltpu.VMEM((2 * slots, count), bf16),
            pltpu.VMEM((2 * slots, count), bf16),
            pltpu.VMEM((2, 4, slots, cols), f32),
            pltpu.VMEM((2, 4, slots, cols), f32),
            dma((3,)), dma((16,)), dma((16,)), dma((16,)), dma((16,)),
            dma((2, 4, 2)), dma((2, 4, 2)),
        ],
        compiler_params=pltpu.CompilerParams(
            collective_id=1 if dense else 0, has_side_effects=True, vmem_limit_bytes=60 * 2**20),
    )(points, centres, white, assign)


def per_device(descriptors, landmarks, whitening, assign):
    return call(256, 256, True, descriptors.T, landmarks.T, whitening, assign.reshape(1, -1))


def solution(mesh):
    placed = (P("rep", "col"), P("row", "col"), P("row", "col"), P())
    return jax.shard_map(
        per_device, mesh=mesh, in_specs=placed, out_specs=P(("row", "rep"), "col"), check_vma=False
    )
```

```python
import functools

import jax
import jax.numpy as jnp
from jax import lax
from jax.experimental import pallas as pl
from jax.experimental.pallas import tpu as pltpu
from jax.sharding import PartitionSpec as P

SPREAD = 51
CLUSTERS = 4096

f32, bf16 = jnp.float32, jnp.bfloat16
MESH = pl.DeviceIdType.MESH


def nn(a, b):
    return lax.dot_general(a, b, (((1,), (0,)), ((), ())), preferred_element_type=f32)


def nt(a, b):
    return lax.dot_general(a, b, (((1,), (1,)), ((), ())), preferred_element_type=f32)


def split(x):
    high = x.astype(bf16)
    return high, (x - high.astype(f32)).astype(bf16)


def ones_where(mask):
    return jnp.where(mask, 1.0, 0.0).astype(bf16)


def iota(shape, axis):
    return lax.broadcasted_iota(jnp.int32, shape, axis)


def kernel(slots, dense, points_ref, centres_ref, white_ref, assign_ref, out_ref,
           lbuf, dbuf, wfull, wh, wl, dh, dl, lh, ll, pick, fold, pos, kh, kl, ah, al,
           sbuf, rbuf, local_sem, gs, gr, fs, fr, zs, zr):
    rows = assign_ref.shape[1]
    part = points_ref.shape[1]
    centres = centres_ref.shape[1]
    cols = white_ref.shape[1]
    owned = out_ref.shape[0]
    half = slots // 2
    z, c, p = lax.axis_index("row"), lax.axis_index("col"), lax.axis_index("rep")
    nz = lax.axis_size("row")
    xh, y, core = c // 8, lax.rem(c // 2, 4), lax.rem(c, 2)
    x = 2 * xh + p

    def device(dx, dy, other=0):
        to = lax.rem(x + dx + 4, 4)
        col = (to // 2) * 8 + lax.rem(y + dy + 4, 4) * 2 + (1 - core if other else core)
        return {"row": z, "col": col, "rep": lax.rem(to, 2)}

    sibling = device(0, 0, 1)
    ahead = {"row": lax.rem(z + 1, nz), "col": c, "rep": p}
    behind = {"row": lax.rem(z + nz - 1, nz), "col": c, "rep": p}

    def d_slot(dx, dy):
        at = lax.rem(x + dx + 4, 4)
        return dbuf.at[at // 2, lax.rem(at, 2), lax.rem(y + dy + 4, 4), core]

    def l_slot(flip, dy):
        return lbuf.at[1 - xh if flip else xh, lax.rem(y + dy + 4, 4), core]

    own_points = pltpu.make_async_copy(points_ref, d_slot(0, 0), local_sem.at[0])
    own_centres = pltpu.make_async_copy(centres_ref, l_slot(0, 0), local_sem.at[1])
    own_white = pltpu.make_async_copy(white_ref, wfull, local_sem.at[2])
    own_points.start()
    own_centres.start()
    own_white.start()

    barrier = pltpu.get_barrier_semaphore()
    near = [sibling, ahead, behind, device(1, 0), device(-1, 0), device(0, 1), device(0, -1)]
    for target in near:
        pl.semaphore_signal(barrier, inc=1, device_id=target, device_id_type=MESH)
    pl.semaphore_wait(barrier, len(near))

    own_points.wait()
    own_centres.wait()

    DIR = (1, -1)
    SIDE = (0, -1, 1, 2)
    ON = ((0, 3), (1, 2))

    def sender(index, ref, target):
        return pltpu.make_async_remote_copy(ref, ref, gs.at[index], gr.at[index], device_id=target, device_id_type=MESH)

    def halves(ref, w):
        return ref.at[:, pl.ds(w * (part // 2), part // 2)]

    moves = {}
    for w in range(2):
        d = DIR[w]
        moves["dy", w] = (w, d_slot(0, 0), device(0, d), d_slot(0, -d))
        moves["dyy", w] = (2 + w, halves(d_slot(0, -d), w), device(0, d), halves(d_slot(0, 2), w))
        for s in range(4):
            moves["dx", w, s] = (4 + w * 4 + s, d_slot(0, SIDE[s]), device(d, 0), d_slot(-d, SIDE[s]))
        for i, s in enumerate(ON[w]):
            moves["dxx", w, s] = (12 + w * 2 + i, d_slot(-d, SIDE[s]), device(d, 0), d_slot(2, SIDE[s]))
        for o in range(2):
            moves["ly", w, o] = (17 + w * 2 + o, l_slot(o, 0), device(0, d), l_slot(o, -d))
        moves["lyy", w] = (21 + w, l_slot(w, -d), device(0, d), l_slot(w, 2))
    moves["lx"] = (16, l_slot(0, 0), device(2 * p - 1, 0), l_slot(1, 0))

    def send(*key):
        index, ref, target, _ = moves[key if len(key) > 1 else key[0]]
        sender(index, ref, target).start()

    def arrive(*key):
        index, _, target, ref = moves[key if len(key) > 1 else key[0]]
        sender(index, ref, target).wait_recv()

    def hand(index, theirs):
        k = 1 - core if theirs else core
        if index < 4:
            ref = lbuf.at[:, lax.rem(y + SIDE[index] + 4, 4), k]
        else:
            at = lax.rem(x + SIDE[index - 4] + 4, 4)
            ref = dbuf.at[at // 2, lax.rem(at, 2), :, k]
        return pltpu.make_async_remote_copy(ref, ref, fs.at[index], fr.at[index], device_id=sibling, device_id_type=MESH)

    for w in range(2):
        send("dy", w)
        send("dx", w, 0)
    send("lx")
    for w in range(2):
        send("ly", w, 0)

    assign = assign_ref[...]
    owner_of = assign // owned

    def owner_at(j):
        far = nz // 2 - (j + 1) // 2
        step = jnp.where(lax.rem(j, 2) == 1, far, nz - far) if not isinstance(j, int) else (far if j % 2 else nz - far)
        return lax.rem(z + step, nz) * 2 + p

    def members(owner):
        return ones_where(iota((owned, rows), 0) == assign - owner * owned)

    if not dense:
        before = ones_where(iota((128, 128), 0) < iota((128, 128), 1))
        base = jnp.zeros((16, 1), f32)
        for block in range(rows // 128):
            at = pl.ds(block * 128, 128)
            mine = ones_where(iota((16, 128), 0) == owner_of[:, block * 128:(block + 1) * 128])
            mine32 = mine.astype(f32)
            pos[:, at] = jnp.sum(mine32 * (nn(mine, before) + base), axis=0, keepdims=True)
            base = base + jnp.sum(mine32, axis=1, keepdims=True)
        below = ones_where(iota((owned, owned), 0) < iota((owned, owned), 1))

    def prepare(j):
        owner = owner_at(j)
        take = fold.shape[2]
        rank = jnp.where(owner_of == owner, pos[...], -1.0).astype(jnp.int32)
        chosen = ones_where(iota((take, rows), 0) == rank)
        pick[j] = chosen
        belongs = members(owner)
        counts = nt(jnp.ones((8, rows), bf16), belongs)
        active = counts > 0.5
        order = nn(ones_where(active), below).astype(jnp.int32)
        squeeze = ones_where((iota((slots, owned), 0) == order[0:1]) & active[0:1])
        fold[j] = nn(squeeze, nt(belongs, chosen).astype(bf16)).astype(bf16)

    def halve_white():
        own_white.wait()

        @pl.loop(0, centres // 128)
        def _(i):
            at = pl.ds(pl.multiple_of(i * 128, 128), 128)
            high, low = split(wfull[at, :])
            wh[at, :] = high
            wl[at, :] = low

    def prepare_pair(j):
        if not dense:
            pl.loop(j, j + 2)(prepare)

    halve_white()
    for w in range(2):
        arrive("dy", w)
        send("dyy", w)
        send("dx", 0, 1 + w)
        send("dx", 1, 1 + w)
    arrive("lx")
    for w in range(2):
        send("ly", w, 1)
    hand(0, False).start()
    prepare_pair(0)
    for w in range(2):
        arrive("ly", w, 0)
    send("lyy", 0)
    for w in range(2):
        arrive("dyy", w)
    for w in range(2):
        send("dx", w, 3)
    hand(4, False).start()
    for w in range(2):
        arrive("dx", w, 0)
    send("dxx", 0, 0)
    prepare_pair(2)
    for s in (1, 2):
        for w in range(2):
            arrive("dx", w, s)
        send("dxx", 1, s)
    for w in range(2):
        arrive("ly", w, 1)
    send("lyy", 1)
    hand(1, False).start()
    hand(2, False).start()
    prepare_pair(4)
    for w in range(2):
        arrive("dx", w, 3)
    send("dxx", 0, 3)
    hand(5, False).start()
    hand(6, False).start()
    for w in range(2):
        arrive("lyy", w)
    hand(3, False).start()
    prepare_pair(6)
    for w in range(2):
        for s in ON[w]:
            arrive("dxx", w, s)
    hand(7, False).start()
    for i in range(4):
        hand(i, True).wait_recv()
    squares = jnp.zeros((1, centres), f32)
    for i in range(2):
        for k in range(4):
            centre = lbuf[i, k]
            squares = squares + jnp.sum((centre * centre).reshape(32, centres), axis=0, keepdims=True)
            lh[i, k], ll[i, k] = split(centre)
    for i in range(4):
        hand(4 + i, True).wait_recv()
    for i in range(2):
        for r in range(2):
            for k in range(4):
                at = pl.ds(r * part, part)
                dh[i, k, :, :, at], dl[i, k, :, :, at] = split(dbuf[i, r, k])

    def flat(ref, lanes=slice(None)):
        value = ref[:, :, :, :, lanes]
        return value.reshape(value.shape[0] * value.shape[1] * value.shape[2] * value.shape[3], value.shape[4])

    def kernel_rows(xhi, xlo, at):
        x = xhi + xlo
        norm = jnp.sum(x * x, axis=1, keepdims=True)
        xhi, xlo = xhi.astype(bf16), xlo.astype(bf16)
        for i in range(centres // 512):
            on = slice(i * 512, (i + 1) * 512)
            inner = nn(xhi, flat(lh, on)) + nn(xhi, flat(ll, on)) + nn(xlo, flat(lh, on))
            value = jnp.exp((norm + squares[:, on] - 2.0 * inner) * (-1.0 / (2.0 * SPREAD)))
            kh[at, on], kl[at, on] = split(value)

    if dense:
        eye = ones_where(iota((256, 256), 0) == iota((256, 256), 1))

        @pl.loop(0, rows // 256)
        def _(i):
            at = pl.ds(pl.multiple_of(i * 256, 256), 256)
            kernel_rows(nt(eye, flat(dh, at)), nt(eye, flat(dl, at)), at)

    def blocks(first, count):
        if not dense:
            take = fold.shape[2]
            for i in range(count):
                chosen = pick[first + i]
                kernel_rows(nt(chosen, flat(dh)), nt(chosen, flat(dl)), slice(i * take, (i + 1) * take))
        for i in range(count):
            at = slice(i * slots, (i + 1) * slots)
            if dense:
                chosen, on = members(owner_at(first + i)), slice(0, rows)
            else:
                chosen, on = fold[first + i], slice(i * take, (i + 1) * take)
            for k in range(centres // 512):
                lanes = slice(k * 512, (k + 1) * 512)
                ah[at, lanes], al[at, lanes] = split(nn(chosen, kh[on, lanes]) + nn(chosen, kl[on, lanes]))
        every = slice(0, count * slots)
        return nn(ah[every, :], wh[...]) + nn(ah[every, :], wl[...]) + nn(al[every, :], wh[...])

    def hop(way, step, part_of):
        at = pl.ds(part_of * half, half)
        return pltpu.make_async_remote_copy(sbuf.at[way, step, at], rbuf.at[way, step, at],
                                            zs.at[way, step, part_of], zr.at[way, step, part_of],
                                            device_id=(ahead, behind)[way], device_id_type=MESH)

    made = blocks(0, 1)
    sbuf[0, 0, :half] = made[:half]
    sbuf[1, 0, half:] = made[half:]
    hop(0, 0, 0).start()
    hop(1, 0, 1).start()
    for step in range(1, 4):
        made = blocks(2 * step - 1, 2)
        sbuf[0, step] = made[:slots]
        sbuf[1, step] = made[slots:]
        for turn in range(2):
            for way in range(2):
                part_of = 1 - way if turn == 0 else way
                at = pl.ds(part_of * half, half)
                if step > 1 or turn == 1:
                    hop(way, step - 1, part_of).wait_recv()
                    sbuf[way, step, at] += rbuf[way, step - 1, at]
                hop(way, step, part_of).start()
    made = blocks(7, 1)
    if not dense:
        belongs = members(lax.rem(z, nz) * 2 + p)
        counts = nn(belongs, jnp.ones((rows, slots), bf16))
        order = nn(ones_where(iota((owned, owned), 0) > iota((owned, owned), 1)), ones_where(counts > 0.5))
        spread = ones_where((order.astype(jnp.int32) == iota((owned, slots), 1)) & (counts > 0.5))
    for way in range(2):
        for part_of in range(2):
            hop(way, 3, part_of).wait_recv()
    total = made + rbuf[0, 3] + rbuf[1, 3]
    if dense:
        out_ref[...] = total
    else:
        high, low = split(total)
        rest = (total - high.astype(f32) - low.astype(f32)).astype(bf16)
        out_ref[...] = nn(spread, high) + nn(spread, low) + nn(spread, rest)

    for index, ref, target, _ in moves.values():
        sender(index, ref, target).wait_send()
    for i in range(8):
        hand(i, False).wait_send()
    for way in range(2):
        for step in range(4):
            for part_of in range(2):
                if step > 0 or part_of == way:
                    hop(way, step, part_of).wait_send()


def call(slots, take, dense, points, centres, white, assign):
    part = points.shape[1]
    count, cols = white.shape
    rows = assign.shape[1]
    owned = CLUSTERS // (lax.axis_size("row") * lax.axis_size("rep"))
    held = rows if dense else 2 * take
    dma = pltpu.SemaphoreType.DMA
    small = dense
    return pl.pallas_call(
        functools.partial(kernel, slots, dense),
        out_shape=jax.ShapeDtypeStruct((owned, cols), f32),
        in_specs=[pl.BlockSpec(memory_space=pl.ANY)] * 3 + [pl.BlockSpec(memory_space=pltpu.VMEM)],
        out_specs=pl.BlockSpec(memory_space=pltpu.VMEM),
        scratch_shapes=[
            pltpu.VMEM((2, 4, 2, 16, count), f32),
            pltpu.VMEM((2, 2, 4, 2, 16, part), f32),
            pltpu.VMEM((count, cols), f32),
            pltpu.VMEM((count, cols), bf16),
            pltpu.VMEM((count, cols), bf16),
            pltpu.VMEM((2, 4, 2, 16, rows), bf16),
            pltpu.VMEM((2, 4, 2, 16, rows), bf16),
            pltpu.VMEM((2, 4, 2, 16, count), bf16),
            pltpu.VMEM((2, 4, 2, 16, count), bf16),
            pltpu.VMEM((8, 16, 128) if small else (8, take, rows), bf16),
            pltpu.VMEM((8, 16, 128) if small else (8, slots, take), bf16),
            pltpu.VMEM((1, rows), f32),
            pltpu.VMEM((held, count), bf16),
            pltpu.VMEM((held, count), bf16),
            pltpu.VMEM((2 * slots, count), bf16),
            pltpu.VMEM((2 * slots, count), bf16),
            pltpu.VMEM((2, 4, slots, cols), f32),
            pltpu.VMEM((2, 4, slots, cols), f32),
            dma((3,)), dma((23,)), dma((23,)), dma((8,)), dma((8,)),
            dma((2, 4, 2)), dma((2, 4, 2)),
        ],
        compiler_params=pltpu.CompilerParams(
            collective_id=1 if dense else 0, has_side_effects=True, vmem_limit_bytes=60 * 2**20),
    )(points, centres, white, assign)


def fits(assign, owners, slots, take):
    high = (assign[None, :] // 64 == jnp.arange(CLUSTERS // 64, dtype=jnp.int32)[:, None]).astype(bf16)
    low = (assign[None, :] % 64 == jnp.arange(64, dtype=jnp.int32)[:, None]).astype(bf16)
    counts = nt(high, low).reshape(owners, -1)
    used = jnp.max(jnp.sum(jnp.minimum(counts, 1.0), axis=1))
    return (used <= slots) & (jnp.max(jnp.sum(counts, axis=1)) <= take)


def per_device(descriptors, landmarks, whitening, assign):
    owners = lax.axis_size("row") * lax.axis_size("rep")
    owned = CLUSTERS // owners
    return lax.cond(
        fits(assign, owners, owned // 2, 256),
        functools.partial(call, owned // 2, 256, False),
        functools.partial(call, owned, 256, True),
        descriptors.T, landmarks.T, whitening, assign.reshape(1, -1))


def solution(mesh):
    placed = (P("rep", "col"), P("row", "col"), P("row", "col"), P())
    return jax.shard_map(
        per_device, mesh=mesh, in_specs=placed, out_specs=P(("row", "rep"), "col"), check_vma=False
    )
```

```python
import functools

import jax
import jax.numpy as jnp
from jax import lax
from jax.experimental import pallas as pl
from jax.experimental.pallas import tpu as pltpu
from jax.sharding import PartitionSpec as P

SPREAD = 51
CLUSTERS = 4096

f32, bf16 = jnp.float32, jnp.bfloat16
MESH = pl.DeviceIdType.MESH


def nn(a, b):
    return lax.dot_general(a, b, (((1,), (0,)), ((), ())), preferred_element_type=f32)


def nt(a, b):
    return lax.dot_general(a, b, (((1,), (1,)), ((), ())), preferred_element_type=f32)


def split(x):
    high = x.astype(bf16)
    return high, (x - high.astype(f32)).astype(bf16)


def ones_where(mask):
    return jnp.where(mask, 1.0, 0.0).astype(bf16)


def iota(shape, axis):
    return lax.broadcasted_iota(jnp.int32, shape, axis)


def kernel(slots, dense, points_ref, centres_ref, white_ref, assign_ref, out_ref, over_ref,
           lbuf, dbuf, wfull, wh, wl, dh, dl, lh, ll, pick, fold, pos, kh, kl, ah, al,
           sbuf, rbuf, local_sem, gs, gr, fs, fr, zs, zr):
    rows = assign_ref.shape[1]
    part = points_ref.shape[1]
    centres = centres_ref.shape[1]
    cols = white_ref.shape[1]
    owned = out_ref.shape[0]
    half = slots // 2
    z, c, p = lax.axis_index("row"), lax.axis_index("col"), lax.axis_index("rep")
    nz = lax.axis_size("row")
    xh, y, core = c // 8, lax.rem(c // 2, 4), lax.rem(c, 2)
    x = 2 * xh + p

    def device(dx, dy, other=0):
        to = lax.rem(x + dx + 4, 4)
        col = (to // 2) * 8 + lax.rem(y + dy + 4, 4) * 2 + (1 - core if other else core)
        return {"row": z, "col": col, "rep": lax.rem(to, 2)}

    sibling = device(0, 0, 1)
    ahead = {"row": lax.rem(z + 1, nz), "col": c, "rep": p}
    behind = {"row": lax.rem(z + nz - 1, nz), "col": c, "rep": p}

    def d_slot(dx, dy):
        at = lax.rem(x + dx + 4, 4)
        return dbuf.at[at // 2, lax.rem(at, 2), lax.rem(y + dy + 4, 4), core]

    def l_slot(flip, dy):
        return lbuf.at[1 - xh if flip else xh, lax.rem(y + dy + 4, 4), core]

    own_points = pltpu.make_async_copy(points_ref, d_slot(0, 0), local_sem.at[0])
    own_centres = pltpu.make_async_copy(centres_ref, l_slot(0, 0), local_sem.at[1])
    own_white = pltpu.make_async_copy(white_ref, wfull, local_sem.at[2])
    own_points.start()
    own_centres.start()
    own_white.start()

    barrier = pltpu.get_barrier_semaphore()
    near = [sibling, ahead, behind, device(1, 0), device(-1, 0), device(0, 1), device(0, -1)]
    for target in near:
        pl.semaphore_signal(barrier, inc=1, device_id=target, device_id_type=MESH)
    pl.semaphore_wait(barrier, len(near))

    own_points.wait()
    own_centres.wait()

    DIR = (1, -1)
    SIDE = (0, -1, 1, 2)
    ON = ((0, 3), (1, 2))

    def sender(index, ref, target):
        return pltpu.make_async_remote_copy(ref, ref, gs.at[index], gr.at[index], device_id=target, device_id_type=MESH)

    def halves(ref, w):
        return ref.at[:, pl.ds(w * (part // 2), part // 2)]

    moves = {}
    for w in range(2):
        d = DIR[w]
        moves["dy", w] = (w, d_slot(0, 0), device(0, d), d_slot(0, -d))
        moves["dyy", w] = (2 + w, halves(d_slot(0, -d), w), device(0, d), halves(d_slot(0, 2), w))
        for s in range(4):
            moves["dx", w, s] = (4 + w * 4 + s, d_slot(0, SIDE[s]), device(d, 0), d_slot(-d, SIDE[s]))
        for i, s in enumerate(ON[w]):
            moves["dxx", w, s] = (12 + w * 2 + i, d_slot(-d, SIDE[s]), device(d, 0), d_slot(2, SIDE[s]))
        for o in range(2):
            moves["ly", w, o] = (17 + w * 2 + o, l_slot(o, 0), device(0, d), l_slot(o, -d))
        moves["lyy", w] = (21 + w, l_slot(w, -d), device(0, d), l_slot(w, 2))
    moves["lx"] = (16, l_slot(0, 0), device(2 * p - 1, 0), l_slot(1, 0))

    def send(*key):
        index, ref, target, _ = moves[key if len(key) > 1 else key[0]]
        sender(index, ref, target).start()

    def arrive(*key):
        index, _, target, ref = moves[key if len(key) > 1 else key[0]]
        sender(index, ref, target).wait_recv()

    def hand(index, theirs):
        k = 1 - core if theirs else core
        if index < 4:
            ref = lbuf.at[:, lax.rem(y + SIDE[index] + 4, 4), k]
        else:
            at = lax.rem(x + SIDE[index - 4] + 4, 4)
            ref = dbuf.at[at // 2, lax.rem(at, 2), :, k]
        return pltpu.make_async_remote_copy(ref, ref, fs.at[index], fr.at[index], device_id=sibling, device_id_type=MESH)

    for w in range(2):
        send("dy", w)
        send("dx", w, 0)
    send("lx")
    for w in range(2):
        send("ly", w, 0)

    assign = assign_ref[...]
    owner_of = assign // owned

    def owner_at(j):
        far = nz // 2 - (j + 1) // 2
        step = jnp.where(lax.rem(j, 2) == 1, far, nz - far) if not isinstance(j, int) else (far if j % 2 else nz - far)
        return lax.rem(z + step, nz) * 2 + p

    def members(owner):
        return ones_where(iota((owned, rows), 0) == assign - owner * owned)

    if not dense:
        before = ones_where(iota((128, 128), 0) < iota((128, 128), 1))
        base = jnp.zeros((16, 1), f32)
        for block in range(rows // 128):
            at = pl.ds(block * 128, 128)
            mine = ones_where(iota((16, 128), 0) == owner_of[:, block * 128:(block + 1) * 128])
            mine32 = mine.astype(f32)
            pos[:, at] = jnp.sum(mine32 * (nn(mine, before) + base), axis=0, keepdims=True)
            base = base + jnp.sum(mine32, axis=1, keepdims=True)
        below = ones_where(iota((owned, owned), 0) < iota((owned, owned), 1))
        counts = nt(ones_where(iota((64, rows), 0) == assign // 64), ones_where(iota((64, rows), 0) == assign % 64))
        group = ones_where(iota((16, 64), 0) == iota((16, 64), 1) // (owned // 64))
        used = jnp.sum(nn(group, ones_where(counts > 0.5)), axis=1, keepdims=True)
        excess = jnp.maximum(used - slots, base - fold.shape[2])
        over_ref[...] = jnp.broadcast_to(jnp.max(excess, axis=0, keepdims=True), over_ref.shape)

    def prepare(j):
        owner = owner_at(j)
        take = fold.shape[2]
        rank = jnp.where(owner_of == owner, pos[...], -1.0).astype(jnp.int32)
        chosen = ones_where(iota((take, rows), 0) == rank)
        pick[j] = chosen
        belongs = members(owner)
        counts = nt(jnp.ones((8, rows), bf16), belongs)
        active = counts > 0.5
        order = nn(ones_where(active), below).astype(jnp.int32)
        squeeze = ones_where((iota((slots, owned), 0) == order[0:1]) & active[0:1])
        fold[j] = nn(squeeze, nt(belongs, chosen).astype(bf16)).astype(bf16)

    def halve_white():
        own_white.wait()

        @pl.loop(0, centres // 128)
        def _(i):
            at = pl.ds(pl.multiple_of(i * 128, 128), 128)
            high, low = split(wfull[at, :])
            wh[at, :] = high
            wl[at, :] = low

    def prepare_at(j):
        if not dense:
            pl.loop(j, j + 1)(prepare)

    def halve_centres(i):
        hand(i, True).wait_recv()
        at = lax.rem(y + SIDE[i] + 4, 4)
        total = jnp.zeros((1, centres), f32)
        for k in range(2):
            centre = lbuf[k, at]
            total = total + jnp.sum((centre * centre).reshape(32, centres), axis=0, keepdims=True)
            lh[k, at], ll[k, at] = split(centre)
        return total

    def halve_points(i):
        hand(4 + i, True).wait_recv()
        at = lax.rem(x + SIDE[i] + 4, 4)
        hi, r = at // 2, lax.rem(at, 2)
        for k in range(4):
            dh[hi, r, k], dl[hi, r, k] = split(dbuf[hi, r, k])

    halve_white()
    for w in range(2):
        arrive("dy", w)
        send("dyy", w)
        send("dx", 0, 1 + w)
        send("dx", 1, 1 + w)
    arrive("lx")
    for w in range(2):
        send("ly", w, 1)
    hand(0, False).start()
    prepare_at(0)
    for w in range(2):
        arrive("dyy", w)
    for w in range(2):
        send("dx", w, 3)
    hand(4, False).start()
    for w in range(2):
        arrive("ly", w, 0)
    send("lyy", 0)
    for w in range(2):
        arrive("dx", w, 0)
    send("dxx", 0, 0)
    prepare_at(1)
    for s in (1, 2):
        for w in range(2):
            arrive("dx", w, s)
        send("dxx", 1, s)
    for w in range(2):
        arrive("ly", w, 1)
    send("lyy", 1)
    hand(1, False).start()
    hand(2, False).start()
    squares = halve_centres(0)
    for w in range(2):
        arrive("dx", w, 3)
    send("dxx", 0, 3)
    hand(5, False).start()
    hand(6, False).start()
    prepare_at(2)
    halve_points(0)
    squares = squares + halve_centres(1)
    squares = squares + halve_centres(2)
    for w in range(2):
        arrive("lyy", w)
    hand(3, False).start()
    halve_points(1)
    halve_points(2)
    for w in range(2):
        for s in ON[w]:
            arrive("dxx", w, s)
    hand(7, False).start()
    squares = squares + halve_centres(3)
    halve_points(3)

    def flat(ref, lanes=slice(None)):
        value = ref[:, :, :, :, lanes]
        return value.reshape(value.shape[0] * value.shape[1] * value.shape[2] * value.shape[3], value.shape[4])

    def points_of(r, ref, lanes=slice(None)):
        value = ref[:, r, :, :, :, lanes]
        return value.reshape(value.shape[0] * value.shape[1] * value.shape[2] * value.shape[3], value.shape[4])

    def picked_points(picked, ref):
        return nt(picked[:, :part], points_of(0, ref)) + nt(picked[:, part:], points_of(1, ref))

    def kernel_rows(xhi, xlo, at):
        x = xhi + xlo
        norm = jnp.sum(x * x, axis=1, keepdims=True)
        xhi, xlo = xhi.astype(bf16), xlo.astype(bf16)
        for i in range(centres // 512):
            on = slice(i * 512, (i + 1) * 512)
            inner = nn(xhi, flat(lh, on)) + nn(xhi, flat(ll, on)) + nn(xlo, flat(lh, on))
            value = jnp.exp((norm + squares[:, on] - 2.0 * inner) * (-1.0 / (2.0 * SPREAD)))
            kh[at, on], kl[at, on] = split(value)

    if dense:
        eye = ones_where(iota((256, 256), 0) == iota((256, 256), 1))

        for r in range(2):
            @pl.loop(0, part // 256)
            def _(i):
                at = pl.ds(pl.multiple_of(i * 256, 256), 256)
                to = pl.ds(pl.multiple_of(r * part + i * 256, 256), 256)
                kernel_rows(nt(eye, points_of(r, dh, at)), nt(eye, points_of(r, dl, at)), to)

    def sum_rows(j, i):
        if dense:
            chosen, on = members(owner_at(j)), slice(0, rows)
        else:
            take = fold.shape[2]
            picked, on = pick[j], slice(i * take, (i + 1) * take)
            kernel_rows(picked_points(picked, dh), picked_points(picked, dl), on)
            chosen = fold[j]
        at = pl.ds(i * slots, slots)

        def lane_tile(lanes):
            ah[at, lanes], al[at, lanes] = split(nn(chosen, kh[on, lanes]) + nn(chosen, kl[on, lanes]))

        if dense:
            @pl.loop(0, centres // 512)
            def _(k):
                lane_tile(pl.ds(pl.multiple_of(k * 512, 512), 512))
        else:
            for k in range(centres // 512):
                lane_tile(slice(k * 512, (k + 1) * 512))

    def blocks(first, count):
        if dense and count > 1:
            @pl.loop(0, count)
            def _(i):
                sum_rows(first + i, i)
        else:
            for i in range(count):
                sum_rows(first + i, i)
        every = slice(0, count * slots)
        return nn(ah[every, :], wh[...]) + nn(ah[every, :], wl[...]) + nn(al[every, :], wh[...])

    def hop(way, step, part_of):
        at = pl.ds(part_of * half, half)
        return pltpu.make_async_remote_copy(sbuf.at[way, step, at], rbuf.at[way, step, at],
                                            zs.at[way, step, part_of], zr.at[way, step, part_of],
                                            device_id=(ahead, behind)[way], device_id_type=MESH)

    made = blocks(0, 1)
    sbuf[0, 0, :half] = made[:half]
    sbuf[1, 0, half:] = made[half:]
    hop(0, 0, 0).start()
    hop(1, 0, 1).start()

    @pl.loop(1, 4)
    def _(step):
        made = blocks(2 * step - 1, 2)
        sbuf[0, step] = made[:slots]
        sbuf[1, step] = made[slots:]
        for turn in range(2):
            for way in range(2):
                part_of = 1 - way if turn == 0 else way
                at = pl.ds(part_of * half, half)

                def join():
                    hop(way, step - 1, part_of).wait_recv()
                    sbuf[way, step, at] += rbuf[way, step - 1, at]

                if turn == 1:
                    join()
                else:
                    pl.when(step > 1)(join)
                hop(way, step, part_of).start()
        if not dense:
            prepare(2 * step + 1)
            pl.when(step < 3)(lambda: prepare(2 * step + 2))

    made = blocks(7, 1)
    if not dense:
        belongs = members(lax.rem(z, nz) * 2 + p)
        counts = nn(belongs, jnp.ones((rows, slots), bf16))
        order = nn(ones_where(iota((owned, owned), 0) > iota((owned, owned), 1)), ones_where(counts > 0.5))
        spread = ones_where((order.astype(jnp.int32) == iota((owned, slots), 1)) & (counts > 0.5))
    for way in range(2):
        for part_of in range(2):
            hop(way, 3, part_of).wait_recv()
    total = made + rbuf[0, 3] + rbuf[1, 3]
    if dense:
        out_ref[...] = total
        over_ref[...] = jnp.zeros_like(over_ref)
    else:
        high, low = split(total)
        rest = (total - high.astype(f32) - low.astype(f32)).astype(bf16)
        out_ref[...] = nn(spread, high) + nn(spread, low) + nn(spread, rest)

    for index, ref, target, _ in moves.values():
        sender(index, ref, target).wait_send()
    for i in range(8):
        hand(i, False).wait_send()
    for way in range(2):
        for step in range(4):
            for part_of in range(2):
                if step > 0 or part_of == way:
                    hop(way, step, part_of).wait_send()


def call(slots, take, dense, points, centres, white, assign):
    part = points.shape[1]
    count, cols = white.shape
    rows = assign.shape[1]
    owned = CLUSTERS // (lax.axis_size("row") * lax.axis_size("rep"))
    held = rows if dense else 2 * take
    dma = pltpu.SemaphoreType.DMA
    small = dense
    return pl.pallas_call(
        functools.partial(kernel, slots, dense),
        out_shape=[jax.ShapeDtypeStruct((owned, cols), f32), jax.ShapeDtypeStruct((8, 128), f32)],
        in_specs=[pl.BlockSpec(memory_space=pl.ANY)] * 3 + [pl.BlockSpec(memory_space=pltpu.VMEM)],
        out_specs=[pl.BlockSpec(memory_space=pltpu.VMEM)] * 2,
        scratch_shapes=[
            pltpu.VMEM((2, 4, 2, 16, count), f32),
            pltpu.VMEM((2, 2, 4, 2, 16, part), f32),
            pltpu.VMEM((count, cols), f32),
            pltpu.VMEM((count, cols), bf16),
            pltpu.VMEM((count, cols), bf16),
            pltpu.VMEM((2, 2, 4, 2, 16, part), bf16),
            pltpu.VMEM((2, 2, 4, 2, 16, part), bf16),
            pltpu.VMEM((2, 4, 2, 16, count), bf16),
            pltpu.VMEM((2, 4, 2, 16, count), bf16),
            pltpu.VMEM((8, 16, 128) if small else (8, take, rows), bf16),
            pltpu.VMEM((8, 16, 128) if small else (8, slots, take), bf16),
            pltpu.VMEM((1, rows), f32),
            pltpu.VMEM((held, count), bf16),
            pltpu.VMEM((held, count), bf16),
            pltpu.VMEM((2 * slots, count), bf16),
            pltpu.VMEM((2 * slots, count), bf16),
            pltpu.VMEM((2, 4, slots, cols), f32),
            pltpu.VMEM((2, 4, slots, cols), f32),
            dma((3,)), dma((23,)), dma((23,)), dma((8,)), dma((8,)),
            dma((2, 4, 2)), dma((2, 4, 2)),
        ],
        compiler_params=pltpu.CompilerParams(
            collective_id=1 if dense else 0, has_side_effects=True, vmem_limit_bytes=60 * 2**20),
    )(points, centres, white, assign)


def per_device(descriptors, landmarks, whitening, assign):
    owned = CLUSTERS // (lax.axis_size("row") * lax.axis_size("rep"))
    args = descriptors.T, landmarks.T, whitening, assign.reshape(1, -1)
    sums, over = call(owned // 2, 256, False, *args)
    return lax.cond(over[0, 0] > 0.5, lambda: call(owned, 256, True, *args)[0], lambda: sums)


def solution(mesh):
    placed = (P("rep", "col"), P("row", "col"), P("row", "col"), P())
    return jax.shard_map(
        per_device, mesh=mesh, in_specs=placed, out_specs=P(("row", "rep"), "col"), check_vma=False
    )
```

```python
import functools

import jax
import jax.numpy as jnp
from jax import lax
from jax.experimental import pallas as pl
from jax.experimental.pallas import tpu as pltpu
from jax.sharding import PartitionSpec as P

SPREAD = 51
CLUSTERS = 4096

f32, bf16 = jnp.float32, jnp.bfloat16
MESH = pl.DeviceIdType.MESH


def nn(a, b):
    return lax.dot_general(a, b, (((1,), (0,)), ((), ())), preferred_element_type=f32)


def nt(a, b):
    return lax.dot_general(a, b, (((1,), (1,)), ((), ())), preferred_element_type=f32)


def split(x):
    high = x.astype(bf16)
    return high, (x - high.astype(f32)).astype(bf16)


def ones_where(mask):
    return jnp.where(mask, 1.0, 0.0).astype(bf16)


def iota(shape, axis):
    return lax.broadcasted_iota(jnp.int32, shape, axis)


def kernel(slots, dense, points_ref, centres_ref, white_ref, assign_ref, out_ref, over_ref,
           lbuf, dbuf, wfull, wh, wl, dh, dl, lh, ll, pick, fold, pos, kh, kl, ah, al,
           sbuf, rbuf, local_sem, gs, gr, fs, fr, zs, zr):
    rows = assign_ref.shape[1]
    part = points_ref.shape[1]
    centres = centres_ref.shape[1]
    cols = white_ref.shape[1]
    owned = out_ref.shape[0]
    half = slots // 2
    z, c, p = lax.axis_index("row"), lax.axis_index("col"), lax.axis_index("rep")
    nz = lax.axis_size("row")
    xh, y, core = c // 8, lax.rem(c // 2, 4), lax.rem(c, 2)
    x = 2 * xh + p

    def device(dx, dy, other=0):
        to = lax.rem(x + dx + 4, 4)
        col = (to // 2) * 8 + lax.rem(y + dy + 4, 4) * 2 + (1 - core if other else core)
        return {"row": z, "col": col, "rep": lax.rem(to, 2)}

    sibling = device(0, 0, 1)
    ahead = {"row": lax.rem(z + 1, nz), "col": c, "rep": p}
    behind = {"row": lax.rem(z + nz - 1, nz), "col": c, "rep": p}

    def d_slot(dx, dy):
        at = lax.rem(x + dx + 4, 4)
        return dbuf.at[at // 2, lax.rem(at, 2), lax.rem(y + dy + 4, 4), core]

    def l_slot(flip, dy):
        return lbuf.at[1 - xh if flip else xh, lax.rem(y + dy + 4, 4), core]

    own_points = pltpu.make_async_copy(points_ref, d_slot(0, 0), local_sem.at[0])
    own_centres = pltpu.make_async_copy(centres_ref, l_slot(0, 0), local_sem.at[1])
    own_white = pltpu.make_async_copy(white_ref, wfull, local_sem.at[2])
    own_points.start()
    own_centres.start()
    own_white.start()

    barrier = pltpu.get_barrier_semaphore()
    near = [sibling, ahead, behind, device(1, 0), device(-1, 0), device(0, 1), device(0, -1), device(0, 2)]
    for target in near:
        pl.semaphore_signal(barrier, inc=1, device_id=target, device_id_type=MESH)
    pl.semaphore_wait(barrier, len(near))

    own_points.wait()
    own_centres.wait()

    DIR = (1, -1)
    SIDE = (0, -1, 1, 2)
    ON = ((0, 3), (1, 2))

    def sender(index, ref, target):
        return pltpu.make_async_remote_copy(ref, ref, gs.at[index], gr.at[index], device_id=target, device_id_type=MESH)

    moves = {}
    for w in range(2):
        d = DIR[w]
        moves["dy", w] = (w, d_slot(0, 0), device(0, d), d_slot(0, -d))
        for s in range(4):
            moves["dx", w, s] = (4 + w * 4 + s, d_slot(0, SIDE[s]), device(d, 0), d_slot(-d, SIDE[s]))
        for i, s in enumerate(ON[w]):
            moves["dxx", w, s] = (12 + w * 2 + i, d_slot(-d, SIDE[s]), device(d, 0), d_slot(2, SIDE[s]))
        for o in range(2):
            moves["ly", w, o] = (17 + w * 2 + o, l_slot(o, 0), device(0, d), l_slot(o, -d))
        moves["lyy", w] = (21 + w, l_slot(w, -d), device(0, d), l_slot(w, 2))
    moves["dyy"] = (2, d_slot(0, 0), device(0, 2), d_slot(0, 2))
    moves["lx"] = (16, l_slot(0, 0), device(2 * p - 1, 0), l_slot(1, 0))

    def send(*key):
        index, ref, target, _ = moves[key if len(key) > 1 else key[0]]
        sender(index, ref, target).start()

    def arrive(*key):
        index, _, target, ref = moves[key if len(key) > 1 else key[0]]
        sender(index, ref, target).wait_recv()

    def hand(index, theirs):
        k = 1 - core if theirs else core
        if index < 4:
            ref = lbuf.at[:, lax.rem(y + SIDE[index] + 4, 4), k]
        else:
            at = lax.rem(x + SIDE[index - 4] + 4, 4)
            ref = dbuf.at[at // 2, lax.rem(at, 2), :, k]
        return pltpu.make_async_remote_copy(ref, ref, fs.at[index], fr.at[index], device_id=sibling, device_id_type=MESH)

    for w in range(2):
        send("dy", w)
        send("dx", w, 0)
    send("dyy")
    send("lx")
    for w in range(2):
        send("ly", w, 0)

    assign = assign_ref[...]
    owner_of = assign // owned

    def owner_at(j):
        far = nz // 2 - (j + 1) // 2
        step = jnp.where(lax.rem(j, 2) == 1, far, nz - far) if not isinstance(j, int) else (far if j % 2 else nz - far)
        return lax.rem(z + step, nz) * 2 + p

    def members(owner):
        return ones_where(iota((owned, rows), 0) == assign - owner * owned)

    if not dense:
        before = ones_where(iota((128, 128), 0) < iota((128, 128), 1))
        base = jnp.zeros((16, 1), f32)
        for block in range(rows // 128):
            at = pl.ds(block * 128, 128)
            mine = ones_where(iota((16, 128), 0) == owner_of[:, block * 128:(block + 1) * 128])
            mine32 = mine.astype(f32)
            pos[:, at] = jnp.sum(mine32 * (nn(mine, before) + base), axis=0, keepdims=True)
            base = base + jnp.sum(mine32, axis=1, keepdims=True)
        below = ones_where(iota((owned, owned), 0) < iota((owned, owned), 1))
        counts = nt(ones_where(iota((64, rows), 0) == assign // 64), ones_where(iota((64, rows), 0) == assign % 64))
        group = ones_where(iota((16, 64), 0) == iota((16, 64), 1) // (owned // 64))
        used = jnp.sum(nn(group, ones_where(counts > 0.5)), axis=1, keepdims=True)
        excess = jnp.maximum(used - slots, base - fold.shape[2])
        over_ref[0, 0] = jnp.max(excess)

    def prepare(j):
        owner = owner_at(j)
        take = fold.shape[2]
        rank = jnp.where(owner_of == owner, pos[...], -1.0).astype(jnp.int32)
        chosen = ones_where(iota((take, rows), 0) == rank)
        pick[j] = chosen
        belongs = members(owner)
        counts = nt(jnp.ones((8, rows), bf16), belongs)
        active = counts > 0.5
        order = nn(ones_where(active), below).astype(jnp.int32)
        squeeze = ones_where((iota((slots, owned), 0) == order[0:1]) & active[0:1])
        fold[j] = nn(squeeze, nt(belongs, chosen).astype(bf16)).astype(bf16)

    def halve_white():
        own_white.wait()

        @pl.loop(0, centres // 128)
        def _(i):
            at = pl.ds(pl.multiple_of(i * 128, 128), 128)
            high, low = split(wfull[at, :])
            wh[at, :] = high
            wl[at, :] = low

    def prepare_at(j):
        if not dense:
            pl.loop(j, j + 1)(prepare)

    def halve_centres(i):
        hand(i, True).wait_recv()
        at = lax.rem(y + SIDE[i] + 4, 4)
        total = jnp.zeros((1, centres), f32)
        for k in range(2):
            centre = lbuf[k, at]
            total = total + jnp.sum((centre * centre).reshape(32, centres), axis=0, keepdims=True)
            lh[k, at], ll[k, at] = split(centre)
        return total

    def halve_points(i):
        hand(4 + i, True).wait_recv()
        at = lax.rem(x + SIDE[i] + 4, 4)
        hi, r = at // 2, lax.rem(at, 2)
        for k in range(4):
            dh[hi, r, k], dl[hi, r, k] = split(dbuf[hi, r, k])

    halve_white()
    for w in range(2):
        arrive("dy", w)
        send("dx", 0, 1 + w)
        send("dx", 1, 1 + w)
    arrive("dyy")
    for w in range(2):
        send("dx", w, 3)
    hand(4, False).start()
    arrive("lx")
    for w in range(2):
        send("ly", w, 1)
    hand(0, False).start()
    prepare_at(0)
    for w in range(2):
        arrive("ly", w, 0)
    send("lyy", 0)
    for w in range(2):
        arrive("dx", w, 0)
    send("dxx", 0, 0)
    prepare_at(1)
    for s in (1, 2):
        for w in range(2):
            arrive("dx", w, s)
        send("dxx", 1, s)
    for w in range(2):
        arrive("ly", w, 1)
    send("lyy", 1)
    hand(1, False).start()
    hand(2, False).start()
    squares = halve_centres(0)
    for w in range(2):
        arrive("dx", w, 3)
    send("dxx", 0, 3)
    hand(5, False).start()
    hand(6, False).start()
    prepare_at(2)
    halve_points(0)
    squares = squares + halve_centres(1)
    squares = squares + halve_centres(2)
    for w in range(2):
        arrive("lyy", w)
    hand(3, False).start()
    halve_points(1)
    halve_points(2)
    for w in range(2):
        for s in ON[w]:
            arrive("dxx", w, s)
    hand(7, False).start()
    squares = squares + halve_centres(3)
    halve_points(3)

    def flat(ref, lanes=slice(None)):
        value = ref[:, :, :, :, lanes]
        return value.reshape(value.shape[0] * value.shape[1] * value.shape[2] * value.shape[3], value.shape[4])

    def points_of(r, ref, lanes=slice(None)):
        value = ref[:, r, :, :, :, lanes]
        return value.reshape(value.shape[0] * value.shape[1] * value.shape[2] * value.shape[3], value.shape[4])

    def picked_points(picked, ref):
        return nt(picked[:, :part], points_of(0, ref)) + nt(picked[:, part:], points_of(1, ref))

    def kernel_rows(xhi, xlo, at):
        x = xhi + xlo
        norm = jnp.sum(x * x, axis=1, keepdims=True)
        xhi, xlo = xhi.astype(bf16), xlo.astype(bf16)
        for i in range(centres // 512):
            on = slice(i * 512, (i + 1) * 512)
            inner = nn(xhi, flat(lh, on)) + nn(xhi, flat(ll, on)) + nn(xlo, flat(lh, on))
            value = jnp.exp((norm + squares[:, on] - 2.0 * inner) * (-1.0 / (2.0 * SPREAD)))
            kh[at, on], kl[at, on] = split(value)

    if dense:
        eye = ones_where(iota((256, 256), 0) == iota((256, 256), 1))

        for r in range(2):
            @pl.loop(0, part // 256)
            def _(i):
                at = pl.ds(pl.multiple_of(i * 256, 256), 256)
                to = pl.ds(pl.multiple_of(r * part + i * 256, 256), 256)
                kernel_rows(nt(eye, points_of(r, dh, at)), nt(eye, points_of(r, dl, at)), to)

    def sum_rows(j, i):
        if dense:
            chosen, on = members(owner_at(j)), slice(0, rows)
        else:
            take = fold.shape[2]
            picked, on = pick[j], slice(i * take, (i + 1) * take)
            kernel_rows(picked_points(picked, dh), picked_points(picked, dl), on)
            chosen = fold[j]
        at = pl.ds(i * slots, slots)

        def lane_tile(lanes):
            ah[at, lanes], al[at, lanes] = split(nn(chosen, kh[on, lanes]) + nn(chosen, kl[on, lanes]))

        if dense:
            @pl.loop(0, centres // 512)
            def _(k):
                lane_tile(pl.ds(pl.multiple_of(k * 512, 512), 512))
        else:
            for k in range(centres // 512):
                lane_tile(slice(k * 512, (k + 1) * 512))

    def blocks(first, count):
        if dense and count > 1:
            @pl.loop(0, count)
            def _(i):
                sum_rows(first + i, i)
        else:
            for i in range(count):
                sum_rows(first + i, i)
        every = slice(0, count * slots)
        return nn(ah[every, :], wh[...]) + nn(ah[every, :], wl[...]) + nn(al[every, :], wh[...])

    def hop(way, step, part_of):
        at = pl.ds(part_of * half, half)
        return pltpu.make_async_remote_copy(sbuf.at[way, step, at], rbuf.at[way, step, at],
                                            zs.at[way, step, part_of], zr.at[way, step, part_of],
                                            device_id=(ahead, behind)[way], device_id_type=MESH)

    made = blocks(0, 1)
    sbuf[0, 0, :half] = made[:half]
    sbuf[1, 0, half:] = made[half:]
    hop(0, 0, 0).start()
    hop(1, 0, 1).start()

    @pl.loop(1, 4)
    def _(step):
        made = blocks(2 * step - 1, 2)
        sbuf[0, step] = made[:slots]
        sbuf[1, step] = made[slots:]
        for turn in range(2):
            for way in range(2):
                part_of = 1 - way if turn == 0 else way
                at = pl.ds(part_of * half, half)

                def join():
                    hop(way, step - 1, part_of).wait_recv()
                    sbuf[way, step, at] += rbuf[way, step - 1, at]

                if turn == 1:
                    join()
                else:
                    pl.when(step > 1)(join)
                hop(way, step, part_of).start()
        if not dense:
            prepare(2 * step + 1)
            pl.when(step < 3)(lambda: prepare(2 * step + 2))

    made = blocks(7, 1)
    if not dense:
        belongs = members(lax.rem(z, nz) * 2 + p)
        counts = nn(belongs, jnp.ones((rows, slots), bf16))
        order = nn(ones_where(iota((owned, owned), 0) > iota((owned, owned), 1)), ones_where(counts > 0.5))
        spread = ones_where((order.astype(jnp.int32) == iota((owned, slots), 1)) & (counts > 0.5))
    for way in range(2):
        for part_of in range(2):
            hop(way, 3, part_of).wait_recv()
    total = made + rbuf[0, 3] + rbuf[1, 3]
    if dense:
        out_ref[...] = total
        over_ref[0, 0] = jnp.float32(0.0)
    else:
        high, low = split(total)
        rest = (total - high.astype(f32) - low.astype(f32)).astype(bf16)
        out_ref[...] = nn(spread, high) + nn(spread, low) + nn(spread, rest)

    for index, ref, target, _ in moves.values():
        sender(index, ref, target).wait_send()
    for i in range(8):
        hand(i, False).wait_send()
    for way in range(2):
        for step in range(4):
            for part_of in range(2):
                if step > 0 or part_of == way:
                    hop(way, step, part_of).wait_send()


def call(slots, take, dense, points, centres, white, assign):
    part = points.shape[1]
    count, cols = white.shape
    rows = assign.shape[1]
    owned = CLUSTERS // (lax.axis_size("row") * lax.axis_size("rep"))
    held = rows if dense else 2 * take
    dma = pltpu.SemaphoreType.DMA
    small = dense
    return pl.pallas_call(
        functools.partial(kernel, slots, dense),
        out_shape=[jax.ShapeDtypeStruct((owned, cols), f32), jax.ShapeDtypeStruct((1, 1), f32)],
        in_specs=[pl.BlockSpec(memory_space=pl.ANY)] * 3 + [pl.BlockSpec(memory_space=pltpu.VMEM)],
        out_specs=[pl.BlockSpec(memory_space=pltpu.VMEM), pl.BlockSpec(memory_space=pltpu.SMEM)],
        scratch_shapes=[
            pltpu.VMEM((2, 4, 2, 16, count), f32),
            pltpu.VMEM((2, 2, 4, 2, 16, part), f32),
            pltpu.VMEM((count, cols), f32),
            pltpu.VMEM((count, cols), bf16),
            pltpu.VMEM((count, cols), bf16),
            pltpu.VMEM((2, 2, 4, 2, 16, part), bf16),
            pltpu.VMEM((2, 2, 4, 2, 16, part), bf16),
            pltpu.VMEM((2, 4, 2, 16, count), bf16),
            pltpu.VMEM((2, 4, 2, 16, count), bf16),
            pltpu.VMEM((8, 16, 128) if small else (8, take, rows), bf16),
            pltpu.VMEM((8, 16, 128) if small else (8, slots, take), bf16),
            pltpu.VMEM((1, rows), f32),
            pltpu.VMEM((held, count), bf16),
            pltpu.VMEM((held, count), bf16),
            pltpu.VMEM((2 * slots, count), bf16),
            pltpu.VMEM((2 * slots, count), bf16),
            pltpu.VMEM((2, 4, slots, cols), f32),
            pltpu.VMEM((2, 4, slots, cols), f32),
            dma((3,)), dma((23,)), dma((23,)), dma((8,)), dma((8,)),
            dma((2, 4, 2)), dma((2, 4, 2)),
        ],
        compiler_params=pltpu.CompilerParams(
            collective_id=1 if dense else 0, has_side_effects=True, vmem_limit_bytes=60 * 2**20),
    )(points, centres, white, assign)


def per_device(descriptors, landmarks, whitening, assign):
    owned = CLUSTERS // (lax.axis_size("row") * lax.axis_size("rep"))
    args = descriptors.T, landmarks.T, whitening, assign.reshape(1, -1)
    sums, over = call(owned // 2, 256, False, *args)
    return lax.cond(over[0, 0] > 0.5, lambda: call(owned, 256, True, *args)[0], lambda: sums)


def solution(mesh):
    placed = (P("rep", "col"), P("row", "col"), P("row", "col"), P())
    return jax.shard_map(
        per_device, mesh=mesh, in_specs=placed, out_specs=P(("row", "rep"), "col"), check_vma=False
    )
```

```python
import functools

import jax
import jax.numpy as jnp
from jax import lax
from jax.experimental import pallas as pl
from jax.experimental.pallas import tpu as pltpu
from jax.sharding import PartitionSpec as P

SPREAD = 51
CLUSTERS = 4096

f32, bf16 = jnp.float32, jnp.bfloat16
MESH = pl.DeviceIdType.MESH


def nn(a, b):
    return lax.dot_general(a, b, (((1,), (0,)), ((), ())), preferred_element_type=f32)


def nt(a, b):
    return lax.dot_general(a, b, (((1,), (1,)), ((), ())), preferred_element_type=f32)


def split(x):
    high = x.astype(bf16)
    return high, (x - high.astype(f32)).astype(bf16)


def ones_where(mask):
    return jnp.where(mask, 1.0, 0.0).astype(bf16)


def iota(shape, axis):
    return lax.broadcasted_iota(jnp.int32, shape, axis)


def kernel(slots, dense, points_ref, centres_ref, white_ref, assign_ref, out_ref, over_ref,
           lbuf, dbuf, wfull, wh, wl, dh, dl, lh, ll, pick, fold, pos, kh, kl, ah, al,
           sbuf, rbuf, local_sem, gs, gr, fs, fr, zs, zr):
    rows = assign_ref.shape[1]
    part = points_ref.shape[1]
    centres = centres_ref.shape[1]
    cols = white_ref.shape[1]
    owned = out_ref.shape[0]
    half = slots // 2
    z, c, p = lax.axis_index("row"), lax.axis_index("col"), lax.axis_index("rep")
    nz = lax.axis_size("row")
    xh, y, core = c // 8, lax.rem(c // 2, 4), lax.rem(c, 2)
    x = 2 * xh + p

    def device(dx, dy, other=0):
        to = lax.rem(x + dx + 4, 4)
        col = (to // 2) * 8 + lax.rem(y + dy + 4, 4) * 2 + (1 - core if other else core)
        return {"row": z, "col": col, "rep": lax.rem(to, 2)}

    sibling = device(0, 0, 1)
    ahead = {"row": lax.rem(z + 1, nz), "col": c, "rep": p}
    behind = {"row": lax.rem(z + nz - 1, nz), "col": c, "rep": p}

    def d_slot(dx, dy):
        at = lax.rem(x + dx + 4, 4)
        return dbuf.at[at // 2, lax.rem(at, 2), lax.rem(y + dy + 4, 4), core]

    def l_slot(flip, dy):
        return lbuf.at[1 - xh if flip else xh, lax.rem(y + dy + 4, 4), core]

    own_points = pltpu.make_async_copy(points_ref, d_slot(0, 0), local_sem.at[0])
    own_centres = pltpu.make_async_copy(centres_ref, l_slot(0, 0), local_sem.at[1])
    own_white = pltpu.make_async_copy(white_ref, wfull, local_sem.at[2])
    own_points.start()
    own_centres.start()
    own_white.start()

    barrier = pltpu.get_barrier_semaphore()
    near = [sibling, ahead, behind, device(1, 0), device(-1, 0), device(0, 1), device(0, -1), device(0, 2)]
    for target in near:
        pl.semaphore_signal(barrier, inc=1, device_id=target, device_id_type=MESH)
    pl.semaphore_wait(barrier, len(near))

    own_points.wait()
    own_centres.wait()

    DIR = (1, -1)
    SIDE = (0, -1, 1, 2)
    ON = ((0, 3), (1, 2))

    def sender(index, ref, target):
        return pltpu.make_async_remote_copy(ref, ref, gs.at[index], gr.at[index], device_id=target, device_id_type=MESH)

    moves = {}
    for w in range(2):
        d = DIR[w]
        moves["dy", w] = (w, d_slot(0, 0), device(0, d), d_slot(0, -d))
        for s in range(4):
            moves["dx", w, s] = (4 + w * 4 + s, d_slot(0, SIDE[s]), device(d, 0), d_slot(-d, SIDE[s]))
        for i, s in enumerate(ON[w]):
            moves["dxx", w, s] = (12 + w * 2 + i, d_slot(-d, SIDE[s]), device(d, 0), d_slot(2, SIDE[s]))
        for o in range(2):
            moves["ly", w, o] = (17 + w * 2 + o, l_slot(o, 0), device(0, d), l_slot(o, -d))
        moves["lyy", w] = (21 + w, l_slot(w, -d), device(0, d), l_slot(w, 2))
    moves["dyy"] = (2, d_slot(0, 0), device(0, 2), d_slot(0, 2))
    moves["lx"] = (16, l_slot(0, 0), device(2 * p - 1, 0), l_slot(1, 0))

    def send(*key):
        index, ref, target, _ = moves[key if len(key) > 1 else key[0]]
        sender(index, ref, target).start()

    def arrive(*key):
        index, _, target, ref = moves[key if len(key) > 1 else key[0]]
        sender(index, ref, target).wait_recv()

    def hand(index, theirs):
        k = 1 - core if theirs else core
        if index < 4:
            ref = lbuf.at[:, lax.rem(y + SIDE[index] + 4, 4), k]
        else:
            at = lax.rem(x + SIDE[index - 4] + 4, 4)
            ref = dbuf.at[at // 2, lax.rem(at, 2), :, k]
        return pltpu.make_async_remote_copy(ref, ref, fs.at[index], fr.at[index], device_id=sibling, device_id_type=MESH)

    for w in range(2):
        send("dy", w)
        send("dx", w, 0)
    send("dyy")
    send("lx")
    for w in range(2):
        send("ly", w, 0)

    assign = assign_ref[...]
    owner_of = assign // owned

    def owner_at(j):
        far = nz // 2 - (j + 1) // 2
        step = jnp.where(lax.rem(j, 2) == 1, far, nz - far) if not isinstance(j, int) else (far if j % 2 else nz - far)
        return lax.rem(z + step, nz) * 2 + p

    def members(owner):
        return ones_where(iota((owned, rows), 0) == assign - owner * owned)

    if not dense:
        before = ones_where(iota((128, 128), 0) < iota((128, 128), 1))
        base = jnp.zeros((16, 1), f32)
        for block in range(rows // 128):
            at = pl.ds(block * 128, 128)
            mine = ones_where(iota((16, 128), 0) == owner_of[:, block * 128:(block + 1) * 128])
            mine32 = mine.astype(f32)
            pos[:, at] = jnp.sum(mine32 * (nn(mine, before) + base), axis=0, keepdims=True)
            base = base + jnp.sum(mine32, axis=1, keepdims=True)
        below = ones_where(iota((owned, owned), 0) < iota((owned, owned), 1))
        counts = nt(ones_where(iota((64, rows), 0) == assign // 64), ones_where(iota((64, rows), 0) == assign % 64))
        group = ones_where(iota((16, 64), 0) == iota((16, 64), 1) // (owned // 64))
        used = jnp.sum(nn(group, ones_where(counts > 0.5)), axis=1, keepdims=True)
        excess = jnp.maximum(used - slots, base - fold.shape[2])
        over_ref[0, 0] = jnp.max(excess)

    def prepare(j):
        owner = owner_at(j)
        take = fold.shape[2]
        rank = jnp.where(owner_of == owner, pos[...], -1.0).astype(jnp.int32)
        chosen = ones_where(iota((take, rows), 0) == rank)
        pick[j] = chosen
        belongs = members(owner)
        counts = nt(jnp.ones((8, rows), bf16), belongs)
        active = counts > 0.5
        order = nn(ones_where(active), below).astype(jnp.int32)
        squeeze = ones_where((iota((slots, owned), 0) == order[0:1]) & active[0:1])
        fold[j] = nn(squeeze, nt(belongs, chosen).astype(bf16)).astype(bf16)

    def halve_white():
        own_white.wait()

        @pl.loop(0, centres // 128)
        def _(i):
            at = pl.ds(pl.multiple_of(i * 128, 128), 128)
            high, low = split(wfull[at, :])
            wh[at, :] = high
            wl[at, :] = low

    def prepare_at(j):
        if not dense:
            pl.loop(j, j + 1)(prepare)

    def halve_centres(i):
        hand(i, True).wait_recv()
        at = lax.rem(y + SIDE[i] + 4, 4)
        total = jnp.zeros((1, centres), f32)
        for k in range(2):
            centre = lbuf[k, at]
            total = total + jnp.sum((centre * centre).reshape(32, centres), axis=0, keepdims=True)
            lh[k, at], ll[k, at] = split(centre)
        return total

    def halve_points(i):
        hand(4 + i, True).wait_recv()
        at = lax.rem(x + SIDE[i] + 4, 4)
        hi, r = at // 2, lax.rem(at, 2)
        for k in range(4):
            dh[hi, r, k], dl[hi, r, k] = split(dbuf[hi, r, k])

    halve_white()
    for w in range(2):
        arrive("dy", w)
        send("dx", 0, 1 + w)
        send("dx", 1, 1 + w)
    arrive("dyy")
    for w in range(2):
        send("dx", w, 3)
    hand(4, False).start()
    arrive("lx")
    for w in range(2):
        send("ly", w, 1)
    hand(0, False).start()
    prepare_at(0)
    for w in range(2):
        arrive("ly", w, 0)
    send("lyy", 0)
    for w in range(2):
        arrive("dx", w, 0)
    send("dxx", 0, 0)
    for s in (1, 2):
        for w in range(2):
            arrive("dx", w, s)
        send("dxx", 1, s)
    for w in range(2):
        arrive("ly", w, 1)
    send("lyy", 1)
    hand(1, False).start()
    hand(2, False).start()
    squares = halve_centres(0)
    for w in range(2):
        arrive("dx", w, 3)
    send("dxx", 0, 3)
    hand(5, False).start()
    hand(6, False).start()
    prepare_at(1)
    halve_points(0)
    squares = squares + halve_centres(1)
    squares = squares + halve_centres(2)
    for w in range(2):
        arrive("lyy", w)
    hand(3, False).start()
    prepare_at(2)
    halve_points(1)
    halve_points(2)
    for w in range(2):
        for s in ON[w]:
            arrive("dxx", w, s)
    hand(7, False).start()
    squares = squares + halve_centres(3)
    halve_points(3)

    def flat(ref, lanes=slice(None)):
        value = ref[:, :, :, :, lanes]
        return value.reshape(value.shape[0] * value.shape[1] * value.shape[2] * value.shape[3], value.shape[4])

    def points_of(r, ref, lanes=slice(None)):
        value = ref[:, r, :, :, :, lanes]
        return value.reshape(value.shape[0] * value.shape[1] * value.shape[2] * value.shape[3], value.shape[4])

    def picked_points(picked, ref):
        return nt(picked[:, :part], points_of(0, ref)) + nt(picked[:, part:], points_of(1, ref))

    def kernel_rows(xhi, xlo, at):
        x = xhi + xlo
        norm = jnp.sum(x * x, axis=1, keepdims=True)
        xhi, xlo = xhi.astype(bf16), xlo.astype(bf16)
        for i in range(centres // 512):
            on = slice(i * 512, (i + 1) * 512)
            inner = nn(xhi, flat(lh, on)) + nn(xhi, flat(ll, on)) + nn(xlo, flat(lh, on))
            value = jnp.exp((norm + squares[:, on] - 2.0 * inner) * (-1.0 / (2.0 * SPREAD)))
            kh[at, on], kl[at, on] = split(value)

    if dense:
        eye = ones_where(iota((256, 256), 0) == iota((256, 256), 1))

        for r in range(2):
            @pl.loop(0, part // 256)
            def _(i):
                at = pl.ds(pl.multiple_of(i * 256, 256), 256)
                to = pl.ds(pl.multiple_of(r * part + i * 256, 256), 256)
                kernel_rows(nt(eye, points_of(r, dh, at)), nt(eye, points_of(r, dl, at)), to)

    def sum_rows(j, i):
        if dense:
            chosen, on = members(owner_at(j)), slice(0, rows)
        else:
            take = fold.shape[2]
            picked, on = pick[j], slice(i * take, (i + 1) * take)
            kernel_rows(picked_points(picked, dh), picked_points(picked, dl), on)
            chosen = fold[j]
        at = pl.ds(i * slots, slots)

        def lane_tile(lanes):
            ah[at, lanes], al[at, lanes] = split(nn(chosen, kh[on, lanes]) + nn(chosen, kl[on, lanes]))

        if dense:
            @pl.loop(0, centres // 512)
            def _(k):
                lane_tile(pl.ds(pl.multiple_of(k * 512, 512), 512))
        else:
            for k in range(centres // 512):
                lane_tile(slice(k * 512, (k + 1) * 512))

    def blocks(first, count):
        if dense and count > 1:
            @pl.loop(0, count)
            def _(i):
                sum_rows(first + i, i)
        else:
            for i in range(count):
                sum_rows(first + i, i)
        every = slice(0, count * slots)
        return nn(ah[every, :], wh[...]) + nn(ah[every, :], wl[...]) + nn(al[every, :], wh[...])

    def hop(way, step, part_of):
        at = pl.ds(part_of * half, half)
        return pltpu.make_async_remote_copy(sbuf.at[way, step, at], rbuf.at[way, step, at],
                                            zs.at[way, step, part_of], zr.at[way, step, part_of],
                                            device_id=(ahead, behind)[way], device_id_type=MESH)

    made = blocks(0, 1)
    sbuf[0, 0, :half] = made[:half]
    sbuf[1, 0, half:] = made[half:]
    hop(0, 0, 0).start()
    hop(1, 0, 1).start()

    @pl.loop(1, 4)
    def _(step):
        made = blocks(2 * step - 1, 2)
        sbuf[0, step] = made[:slots]
        sbuf[1, step] = made[slots:]
        for turn in range(2):
            for way in range(2):
                part_of = 1 - way if turn == 0 else way
                at = pl.ds(part_of * half, half)

                def join():
                    hop(way, step - 1, part_of).wait_recv()
                    sbuf[way, step, at] += rbuf[way, step - 1, at]

                if turn == 1:
                    join()
                else:
                    pl.when(step > 1)(join)
                hop(way, step, part_of).start()
        if not dense:
            prepare(2 * step + 1)
            pl.when(step < 3)(lambda: prepare(2 * step + 2))

    made = blocks(7, 1)
    if not dense:
        belongs = members(lax.rem(z, nz) * 2 + p)
        counts = nn(belongs, jnp.ones((rows, slots), bf16))
        order = nn(ones_where(iota((owned, owned), 0) > iota((owned, owned), 1)), ones_where(counts > 0.5))
        spread = ones_where((order.astype(jnp.int32) == iota((owned, slots), 1)) & (counts > 0.5))
    for way in range(2):
        for part_of in range(2):
            hop(way, 3, part_of).wait_recv()
    total = made + rbuf[0, 3] + rbuf[1, 3]
    if dense:
        out_ref[...] = total
        over_ref[0, 0] = jnp.float32(0.0)
    else:
        high, low = split(total)
        rest = (total - high.astype(f32) - low.astype(f32)).astype(bf16)
        out_ref[...] = nn(spread, high) + nn(spread, low) + nn(spread, rest)

    for index, ref, target, _ in moves.values():
        sender(index, ref, target).wait_send()
    for i in range(8):
        hand(i, False).wait_send()
    for way in range(2):
        for step in range(4):
            for part_of in range(2):
                if step > 0 or part_of == way:
                    hop(way, step, part_of).wait_send()


def call(slots, take, dense, points, centres, white, assign):
    part = points.shape[1]
    count, cols = white.shape
    rows = assign.shape[1]
    owned = CLUSTERS // (lax.axis_size("row") * lax.axis_size("rep"))
    held = rows if dense else 2 * take
    dma = pltpu.SemaphoreType.DMA
    small = dense
    return pl.pallas_call(
        functools.partial(kernel, slots, dense),
        out_shape=[jax.ShapeDtypeStruct((owned, cols), f32), jax.ShapeDtypeStruct((1, 1), f32)],
        in_specs=[pl.BlockSpec(memory_space=pl.ANY)] * 3 + [pl.BlockSpec(memory_space=pltpu.VMEM)],
        out_specs=[pl.BlockSpec(memory_space=pltpu.VMEM), pl.BlockSpec(memory_space=pltpu.SMEM)],
        scratch_shapes=[
            pltpu.VMEM((2, 4, 2, 16, count), f32),
            pltpu.VMEM((2, 2, 4, 2, 16, part), f32),
            pltpu.VMEM((count, cols), f32),
            pltpu.VMEM((count, cols), bf16),
            pltpu.VMEM((count, cols), bf16),
            pltpu.VMEM((2, 2, 4, 2, 16, part), bf16),
            pltpu.VMEM((2, 2, 4, 2, 16, part), bf16),
            pltpu.VMEM((2, 4, 2, 16, count), bf16),
            pltpu.VMEM((2, 4, 2, 16, count), bf16),
            pltpu.VMEM((8, 16, 128) if small else (8, take, rows), bf16),
            pltpu.VMEM((8, 16, 128) if small else (8, slots, take), bf16),
            pltpu.VMEM((1, rows), f32),
            pltpu.VMEM((held, count), bf16),
            pltpu.VMEM((held, count), bf16),
            pltpu.VMEM((2 * slots, count), bf16),
            pltpu.VMEM((2 * slots, count), bf16),
            pltpu.VMEM((2, 4, slots, cols), f32),
            pltpu.VMEM((2, 4, slots, cols), f32),
            dma((3,)), dma((23,)), dma((23,)), dma((8,)), dma((8,)),
            dma((2, 4, 2)), dma((2, 4, 2)),
        ],
        compiler_params=pltpu.CompilerParams(
            collective_id=1 if dense else 0, has_side_effects=True, vmem_limit_bytes=60 * 2**20),
    )(points, centres, white, assign)


def per_device(descriptors, landmarks, whitening, assign):
    owned = CLUSTERS // (lax.axis_size("row") * lax.axis_size("rep"))
    args = descriptors.T, landmarks.T, whitening, assign.reshape(1, -1)
    sums, over = call(owned // 2, 256, False, *args)
    return lax.cond(over[0, 0] > 0.5, lambda: call(owned, 256, True, *args)[0], lambda: sums)


def solution(mesh):
    placed = (P("rep", "col"), P("row", "col"), P("row", "col"), P())
    return jax.shard_map(
        per_device, mesh=mesh, in_specs=placed, out_specs=P(("row", "rep"), "col"), check_vma=False
    )
```
